32 devices in a mesh: group: 4 (over z), tensor: 8 (over y, x, core).
Axes of the slice: x: 2, y: 2, z: 4, core: 2. Of those that a mesh axis runs over, the one named last changes fastest.
Arguments:
- low_state: bfloat16 [2048, 8192], P('group', 'tensor'), may hold values from -6 to 6
- mid_state: bfloat16 [2048, 8192], P('group', 'tensor'), may hold values from -6 to 6
- residual: bfloat16 [2048, 8192], P('group', 'tensor'), may hold values from -6 to 6
- attention: bfloat16 [2048, 8192], P('group', 'tensor'), may hold values from -6 to 6
- o_weight: bfloat16 [8192, 8192], P('tensor'), may hold values from -0.0625 to 0.0625
- fc_weight: bfloat16 [3, 8192, 8192], P(None, 'tensor', 'group'), may hold values from -0.0390625 to 0.0390625
- norm_gain: float32 [8192], P('group'), may hold values from 0.1 to 1.9
- target: bfloat16 [512, 8192], P('tensor', 'group'), may hold values from -6 to 6
- counts: int32 [4], replicated, may hold values from 32 to 128, as said below
- accept_rows: int32 [4, 512], replicated, may hold values from 0 to 511, each once within a row
- owners: int32 [4, 512], replicated, may hold values from 0 to 3, as said below
Outputs:
- top_state: bfloat16 [2048, 8192], P('group', 'tensor')
- fc_grad: float32 [3, 8192, 8192], P(None, 'tensor', 'group')
The draws below stay inside these ranges and needn't reach their ends.
Inputs may be any that keep to these rules, and one draw needn't show every extreme that they name: The counts sum to exactly 256. Every replica accepts at least 32 rows, and in every draw one replica accepts 4 * 32. `accept_rows`: only the first counts[g] entries of row g are accepted rows. `owners`: among the first counts[g] entries of row g no shard appears more than 32 times; in every draw one shard receives exactly 32 rows from every replica, and the replica with the most accepted rows sends 32 to every shard. Later entries are unused.
All inputs are finite; a program needn't handle non-finite values.
Results may differ from the reference program's by a relative error of at most 0.012.
Values may be sent and summed in bfloat16 or wider, within the bound.
No kernel may reach another device: no remote copies, remote signals or barrier semaphores. Data moves between devices by JAX's collectives and lax.ppermute only.
A program may use at most 128 MiB of HBM per device.

```python
import jax
import jax.numpy as jnp
from jax import lax

D = 8192
ROWS = 512
SLOTS = 32
ALL_ROWS = 2048
TRAIN_ROWS = 512
ACCEPTED = 256
N_GROUP = 4
N_TENSOR = 8


def routing_draw(key):
    base = jax.random.fold_in(key, 4711)
    keys = jax.random.split(base, 4)
    length = N_GROUP * SLOTS
    busiest = jax.random.randint(keys[1], (), 0, N_GROUP)
    is_busiest = jnp.arange(N_GROUP) == busiest
    weights = jnp.where(is_busiest, 0, jax.random.randint(keys[0], (N_GROUP,), 1, 3)).astype(jnp.int32)
    spare = ACCEPTED - length - (N_GROUP - 1) * SLOTS
    running = jnp.cumsum(weights).astype(jnp.int32)
    bounds = spare * running // running[-1]
    extras = bounds - jnp.concatenate([jnp.zeros((1,), jnp.int32), bounds[:-1]])
    counts = jnp.where(is_busiest, length, SLOTS + extras).astype(jnp.int32)
    full_owner = jax.random.randint(keys[2], (), 0, N_GROUP)
    labels = jnp.repeat(jnp.arange(N_GROUP, dtype=jnp.int32), SLOTS)
    position = jnp.arange(length, dtype=jnp.int32)

    def one_replica(replica_key, accepted):
        first_key, second_key, third_key = jax.random.split(replica_key, 3)
        noise = jax.random.randint(first_key, (length,), 1, 4096)
        score = jnp.where(labels == full_owner, 0, noise) * length + position
        ordered = labels[jnp.argsort(score)]
        mixing = jax.random.randint(second_key, (length,), 0, 4096)
        order_key = jnp.where(position < accepted, mixing, 4096) * length + position
        shuffled = ordered[jnp.argsort(order_key)]
        remainder = jax.random.randint(third_key, (ROWS - length,), 0, N_GROUP)
        return jnp.concatenate([shuffled, remainder.astype(jnp.int32)]).astype(jnp.int32)
    owners = jax.vmap(one_replica)(jax.random.split(keys[3], N_GROUP), counts)
    return (counts, owners)


def draw_counts(key, part):
    return routing_draw(key)[0]


def draw_owners(key, part):
    return routing_draw(key)[1]


def block_scale(stream_key, extent, pieces, low, top_value):
    loudness = 1.0
    for dim, blocks in pieces:
        heights = jax.random.uniform(jax.random.fold_in(jax.random.fold_in(stream_key, 6), dim), (blocks,), jnp.float32, low / len(pieces), top_value / len(pieces))
        loudness = loudness * jnp.repeat(jnp.exp(heights), extent[dim] // blocks).reshape((-1,) + (1,) * (len(extent) - 1 - dim))
    return loudness


def bell_draw(rng, shape, spread, limit, cuts=(), held_as=jnp.bfloat16):
    array = spread * jax.random.normal(rng, shape, jnp.float32)
    if cuts:
        array = array * block_scale(rng, shape, cuts, -0.22, 0.18)
    return jnp.clip(array, -limit, limit).astype(held_as)


def setup_inputs(seed: int = 0) -> dict:
    seeds = jax.random.split(jax.random.key(seed), 12)
    return {
        "low_state": bell_draw(seeds[0], (ALL_ROWS, D), 1.0, 6.0, ((0, 4), (1, 8))),
        "mid_state": bell_draw(seeds[1], (ALL_ROWS, D), 1.0, 6.0, ((0, 4), (1, 8))),
        "residual": bell_draw(seeds[2], (ALL_ROWS, D), 1.0, 6.0, ((0, 4), (1, 8))),
        "attention": bell_draw(seeds[3], (ALL_ROWS, D), 1.0, 6.0, ((0, 4), (1, 8))),
        "o_weight": bell_draw(seeds[4], (D, D), D ** -0.5, 0.0625, ((0, 8),)),
        "fc_weight": bell_draw(seeds[5], (3, D, D), (3 * D) ** -0.5, 0.0390625, ((1, 8), (2, 4))),
        "norm_gain": jnp.clip(1.0 + 0.18 * jax.random.normal(seeds[6], (D,), jnp.float32), 0.1, 1.9),
        "target": bell_draw(seeds[7], (TRAIN_ROWS, D), 1.0, 6.0, ((0, 8), (1, 4))),
        "counts": draw_counts(jax.random.fold_in(seeds[11], 71), 0),
        "accept_rows": jax.vmap(lambda own: jax.random.permutation(own, ROWS))(jax.random.split(seeds[9], N_GROUP)).reshape((N_GROUP, ROWS)).astype(jnp.int32),
        "owners": draw_owners(jax.random.fold_in(seeds[11], 71), 0),
    }


epsilon = 1e-05

def reference(low_state, mid_state, residual, attention, o_weight, fc_weight, norm_gain, target, counts, accept_rows, owners):
    width = D // N_TENSOR
    partial_total = jnp.zeros((N_GROUP * ROWS, D), jnp.float32)
    for block in range(N_TENSOR):
        term = jnp.dot(attention[:, block * width:(block + 1) * width], o_weight[block * width:(block + 1) * width], preferred_element_type=jnp.float32)
        rounded = lax.optimization_barrier(term.astype(jnp.bfloat16))
        partial_total = partial_total + rounded.astype(jnp.float32)
    top_state = (residual.astype(jnp.float32) + partial_total).astype(jnp.bfloat16)
    capacity = N_GROUP * SLOTS
    train_rows = N_GROUP * capacity
    live = jnp.arange(ROWS, dtype=jnp.int32)[None, :] < counts[:, None]
    onehot = ((owners[:, :, None] == jnp.arange(N_GROUP, dtype=jnp.int32)[None, None, :]) & live[:, :, None]).astype(jnp.int32)
    ranks = lax.optimization_barrier(jnp.sum((jnp.cumsum(onehot, axis=1) - onehot) * onehot, axis=2))
    replica = jnp.arange(N_GROUP, dtype=jnp.int32)[:, None]
    slot = jnp.where(live, owners * capacity + replica * SLOTS + ranks, train_rows).astype(jnp.int32)
    whole_row = (replica * ROWS + accept_rows).astype(jnp.int32)
    source = jnp.zeros((train_rows + 1,), jnp.int32).at[slot.reshape(-1)].set(whole_row.reshape(-1))[:train_rows]
    valid = jnp.zeros((train_rows + 1,), jnp.float32).at[slot.reshape(-1)].set(1.0)[:train_rows]
    states = jnp.concatenate([low_state, mid_state, top_state], axis=1)
    inputs = jnp.take(states, source, axis=0) * valid[:, None].astype(jnp.bfloat16)
    combined = jnp.dot(inputs, fc_weight.reshape(3 * D, D), preferred_element_type=jnp.float32)
    squares = lax.optimization_barrier(jnp.sum(combined * combined, axis=1))
    scale = lax.rsqrt(squares / D + epsilon)
    gain = norm_gain.astype(jnp.float32)
    normed = combined * scale[:, None] * gain[None, :]
    total = jnp.sum(counts).astype(jnp.float32)
    slope = valid[:, None] * (normed - target.astype(jnp.float32)) / total
    inner = lax.optimization_barrier(jnp.sum(gain[None, :] * slope * combined, axis=1))
    back = scale[:, None] * gain[None, :] * slope - combined * (scale ** 3 * inner / D)[:, None]
    back = back.astype(jnp.bfloat16)
    grad = jnp.dot(inputs.T, back, preferred_element_type=jnp.float32)
    return (top_state, grad.reshape(3, D, D))
```

```python
import functools

import jax
import jax.numpy as jnp
from jax import lax
from jax.experimental import pallas as pl
from jax.experimental.pallas import tpu as pltpu
from jax.sharding import PartitionSpec as P

epsilon = 1e-05
f32 = jnp.float32
bf16 = jnp.bfloat16


def matmul_blocks_kernel(order_ref, x_ref, w_ref, o_ref):
    o_ref[0] = jnp.dot(x_ref[...], w_ref[...], preferred_element_type=f32).astype(bf16)


def matmul_blocks(x, w, order, width):
    rows, depth = x.shape
    blocks = order.shape[0]
    return pl.pallas_call(
        matmul_blocks_kernel,
        grid_spec=pltpu.PrefetchScalarGridSpec(
            num_scalar_prefetch=1,
            grid=(blocks,),
            in_specs=[
                pl.BlockSpec((rows, depth), lambda j, o: (0, 0)),
                pl.BlockSpec((depth, width), lambda j, o: (0, o[j])),
            ],
            out_specs=pl.BlockSpec((1, rows, width), lambda j, o: (j, 0, 0)),
        ),
        out_shape=jax.ShapeDtypeStruct((blocks, rows, width), bf16),
        cost_estimate=pl.CostEstimate(
            flops=2 * rows * depth * width * blocks,
            bytes_accessed=2 * (rows * depth + depth * width * blocks + rows * width * blocks),
            transcendentals=0,
        ),
    )(order, x, w)


def shards(
    low_state,
    mid_state,
    residual,
    attention,
    o_weight,
    fc_weight,
    norm_gain,
    target,
    counts,
    accept_rows,
    owners,
):
    groups = lax.axis_size("group")
    tensors = lax.axis_size("tensor")
    g = lax.axis_index("group")
    t = lax.axis_index("tensor")
    core = t % 2
    chips = tensors // 2
    rows, width = low_state.shape
    out_features = fc_weight.shape[2]
    share = target.shape[0]
    train_rows = share * tensors
    slots = train_rows // (groups * groups)
    cap = groups * slots
    accepted = train_rows // 2
    half = accepted // 2

    def swap(x, mask):
        return lax.ppermute(x, "tensor", [(i, i ^ mask) for i in range(tensors)])

    def shift(x, k):
        return lax.ppermute(x, "group", [(i, (i + k) % groups) for i in range(groups)])

    def dot(a, b):
        return jnp.dot(a, b, preferred_element_type=f32)

    my_rows = lax.dynamic_index_in_dim(accept_rows, g, 0, keepdims=False)
    my_count = lax.dynamic_index_in_dim(counts, g, 0, keepdims=False)
    pick = (my_rows[:, None] == jnp.arange(rows, dtype=jnp.int32)[None, :]).astype(bf16)
    pick_acc = pick[:cap]
    pick_rest = pick[cap:]

    low_acc = dot(pick_acc, low_state).astype(bf16)
    mid_acc = dot(pick_acc, mid_state).astype(bf16)
    early = jnp.stack([low_acc, mid_acc])
    early_all = [early] + [shift(early, k) for k in range(1, groups)]

    chip_order = 2 * jnp.arange(chips, dtype=jnp.int32)
    give_order = t ^ (chip_order + 1)
    keep_order = t ^ chip_order

    att_acc = dot(pick_acc, attention).astype(bf16)
    give = matmul_blocks(att_acc, o_weight, give_order, width)
    got = swap(give, 1)
    keep = matmul_blocks(att_acc, o_weight, keep_order, width)
    res_acc = dot(pick_acc, residual)
    both = keep.astype(f32) + got.astype(f32)
    top_acc = res_acc + both[0]
    for m in range(1, chips):
        top_acc = top_acc + swap(both[m].astype(bf16), 2 * m).astype(f32)
    top_acc = top_acc.astype(bf16)
    top_all = [top_acc] + [shift(top_acc, k) for k in range(1, groups)]

    att_rest = dot(pick_rest, attention).astype(bf16)
    give_r = matmul_blocks(att_rest, o_weight, give_order, width)
    got_r = swap(give_r, 1)
    keep_r = matmul_blocks(att_rest, o_weight, keep_order, width)
    both_r = (keep_r.astype(f32) + got_r.astype(f32)).astype(bf16)
    n_rest = rows - cap
    bits = [1 << i for i in range(1, tensors.bit_length() - 1)]
    sums = []
    for part, order in enumerate((bits, bits[::-1])):
        lo = part * (n_rest // 2)
        held = {2 * m: both_r[m, lo : lo + n_rest // 2] for m in range(chips)}
        for bit in order:
            going = sorted(j for j in held if j & bit)
            came = swap(jnp.stack([held[j] for j in going]), bit)
            held = {
                j ^ bit: (held[j ^ bit].astype(f32) + came[i].astype(f32)).astype(bf16)
                for i, j in enumerate(going)
            }
        sums.append(held[0])
    res_rest = dot(pick_rest, residual)
    top_rest = (res_rest + jnp.concatenate(sums).astype(f32)).astype(bf16)
    top_perm = jnp.concatenate([top_acc, top_rest])
    top_state = lax.dot_general(
        pick, top_perm, (((0,), (0,)), ((), ())), preferred_element_type=f32
    ).astype(bf16)

    ends = jnp.sum(
        jnp.where(
            jnp.arange(groups)[None, :] <= jnp.arange(groups)[:, None], counts[None, :], 0
        ),
        axis=1,
    ).astype(jnp.int32)
    starts = ends - counts
    position = (jnp.arange(accepted, dtype=jnp.int32) + core * half) % accepted
    from_replica = (g - jnp.arange(groups, dtype=jnp.int32)) % groups
    k = jnp.arange(cap, dtype=jnp.int32)

    def places(replicas):
        at = starts[replicas][:, None] + k[None, :]
        return jnp.where(k[None, :] < counts[replicas][:, None], at, -1).reshape(-1)

    compact = (position[:, None] == places(from_replica)[None, :]).astype(bf16)

    early_rows = jnp.concatenate(early_all, axis=1)
    low_c = dot(compact, early_rows[0]).astype(bf16)
    mid_c = dot(compact, early_rows[1]).astype(bf16)
    top_c = dot(compact, jnp.concatenate(top_all)).astype(bf16)
    combined = dot(low_c, fc_weight[0]) + dot(mid_c, fc_weight[1]) + dot(top_c, fc_weight[2])

    own = owners[:, :cap]
    earlier = k[None, :] < k[:, None]
    ranks = jnp.sum(
        ((own[:, None, :] == own[:, :, None]) & earlier[None]).astype(jnp.int32), axis=2
    )
    slot = own * cap + jnp.arange(groups, dtype=jnp.int32)[:, None] * slots + ranks
    slot_at = places(jnp.arange(groups, dtype=jnp.int32))
    slot_of = jnp.sum(
        jnp.where(position[:, None] == slot_at[None, :], slot.reshape(-1)[None, :], 0), axis=1
    )
    targets = jnp.concatenate([target] + [swap(target, 2 * m) for m in range(1, chips)])
    held_slots = (
        (t ^ chip_order)[:, None] * share + jnp.arange(share, dtype=jnp.int32)[None, :]
    ).reshape(-1)
    target_pick = (slot_of[:, None] == held_slots[None, :]).astype(bf16)
    picked = dot(target_pick, targets).astype(bf16)
    goal = picked[:half].astype(f32) + swap(picked[half:], 1).astype(f32)

    mine = combined[:half] + swap(combined[half:].astype(bf16), 1).astype(f32)
    parts = []
    for part, order in enumerate((bits, bits[::-1])):
        lo = part * (out_features // 2)
        piece = mine[:, lo : lo + out_features // 2]
        for bit in order:
            piece = piece + swap(piece.astype(bf16), bit).astype(f32)
        parts.append(piece)
    c = jnp.concatenate(parts, axis=1)

    gain = norm_gain.astype(f32)[None, :]
    gc = gain * c
    stats = jnp.stack(
        [jnp.sum(c * c, axis=1), jnp.sum(gc * gc, axis=1), jnp.sum(gc * goal, axis=1)]
    )
    whole = stats
    for s in range(1, groups):
        whole = whole + shift(stats, s)
    features = out_features * groups
    total = jnp.sum(counts).astype(f32)
    scale = lax.rsqrt(whole[0] / features + epsilon)
    inner = (scale * whole[1] - whole[2]) / total
    slope = (gc * scale[:, None] - goal) / total
    back = scale[:, None] * gain * slope - c * (scale**3 * inner / features)[:, None]
    back = back.astype(bf16)
    backs = jnp.concatenate([back, swap(back, 1)])
    inputs = jnp.concatenate([low_c, mid_c, top_c], axis=1)
    grad = lax.dot_general(
        inputs, backs, (((0,), (0,)), ((), ())), preferred_element_type=f32
    )
    return (top_state, grad.reshape(fc_weight.shape))


def solution(mesh):
    in_specs = (
        P("group", "tensor"),
        P("group", "tensor"),
        P("group", "tensor"),
        P("group", "tensor"),
        P("tensor", None),
        P(None, "tensor", "group"),
        P("group"),
        P("tensor", "group"),
        P(),
        P(),
        P(),
    )
    out_specs = (P("group", "tensor"), P(None, "tensor", "group"))
    return jax.shard_map(shards, mesh=mesh, in_specs=in_specs, out_specs=out_specs, check_vma=False)
```

```python
import functools

import jax
import jax.numpy as jnp
from jax import lax
from jax.experimental import pallas as pl
from jax.experimental.pallas import tpu as pltpu
from jax.sharding import PartitionSpec as P


epsilon = 1e-05
f32 = jnp.float32
bf16 = jnp.bfloat16
i32 = jnp.int32


VMEM = pl.BlockSpec(memory_space=pltpu.VMEM)
SMEM = pl.BlockSpec(memory_space=pltpu.SMEM)
HBM = pl.BlockSpec(memory_space=pltpu.HBM)


def iota(shape, dim):
    return lax.broadcasted_iota(i32, shape, dim)


def cost(flops, read):
    return pl.CostEstimate(flops=int(flops), bytes_accessed=int(read), transcendentals=0)


def params(mib=56):
    return pltpu.CompilerParams(vmem_limit_bytes=mib << 20)


def in_hbm(*arrays):
    return [pltpu.with_memory_space_constraint(x, pltpu.HBM) for x in arrays]


def fetch_all(pairs, sems):
    copies = [
        pltpu.make_async_copy(src, dst, sems.at[i]) for i, (src, dst) in enumerate(pairs)
    ]
    for copy in copies:
        copy.start()
    return copies


def hit(cond):
    return jnp.where(cond, 1.0, 0.0).astype(bf16)


def place_of(rows_ref, lo, hi, replica):
    groups, rows = rows_ref.shape
    ids = jnp.where(iota((groups, hi - lo), 0) == replica, rows_ref[:, lo:hi], 0)
    ids = jnp.sum(ids, axis=0, keepdims=True)
    return hit(iota((rows, hi - lo), 0) == ids)


def pick_rows(place, x):
    return lax.dot_general(
        place, x, (((0,), (0,)), ((), ())), preferred_element_type=f32
    ).astype(bf16)


def early_kernel(rows_ref, low_ref, mid_ref, *refs):
    *outs, ids, buf, sem = refs
    copies = fetch_all([(rows_ref, ids), (low_ref, buf.at[0]), (mid_ref, buf.at[1])], sem)
    copies[0].wait()
    place = place_of(ids, 0, outs[0].shape[1], lax.axis_index("group"))
    for i in range(2):
        copies[1 + i].wait()
        got = pick_rows(place, buf[i])
        for out in outs:
            out[i] = got[: out.shape[1]]


def early_rows(accept_rows, low, mid, common, cap):
    rows, width = low.shape
    shapes = [(2, cap, width)] + ([(2, common, width)] if cap > common else [])
    return pl.pallas_call(
        early_kernel,
        in_specs=[HBM] * 3,
        out_specs=[VMEM] * len(shapes),
        out_shape=[jax.ShapeDtypeStruct(s, bf16) for s in shapes],
        scratch_shapes=[
            pltpu.VMEM(accept_rows.shape, i32),
            pltpu.VMEM((2, rows, width), bf16),
            pltpu.SemaphoreType.DMA((3,)),
        ],
        compiler_params=params(8),
        cost_estimate=cost(4 * rows * width * cap, 4 * rows * width + 4 * cap * width),
        name="early_rows",
    )(*in_hbm(accept_rows, low, mid))


def project_kernel(
    chip_order,
    cap,
    rows_ref,
    att_ref,
    res_ref,
    w_ref,
    give_acc,
    keep_acc,
    res_acc,
    give_rest,
    keep_rest,
    res_rest,
    ids,
    att,
    res,
    picked,
    wbuf,
    obuf,
    sem,
    small_sem,
):
    chips = len(chip_order)
    width = wbuf.shape[2]
    rows = att.shape[0]
    t = lax.axis_index("tensor")

    def fetch(i, block):
        at = pl.ds(pl.multiple_of((t ^ block) * width, 128), width)
        return pltpu.make_async_copy(w_ref.at[:, at], wbuf.at[i], sem.at[0, i])

    def put(i):
        j = i % chips
        rest = give_rest if i < chips else keep_rest
        copies = [
            pltpu.make_async_copy(
                obuf.at[i, pl.ds(cap, rows - cap)], rest.at[j], sem.at[1, i]
            )
        ]
        if i < chips:
            copies.append(
                pltpu.make_async_copy(
                    obuf.at[i, pl.ds(0, cap)], give_acc.at[j], sem.at[2, i]
                )
            )
        return copies

    order = [2 * m + 1 for m in chip_order] + [2 * m for m in chip_order]
    ahead = 3
    copies = fetch_all([(rows_ref, ids), (att_ref, att)], small_sem)
    late = pltpu.make_async_copy(res_ref, res, small_sem.at[2])
    for i in range(ahead):
        fetch(i, order[i]).start()
    copies[0].wait()
    place = place_of(ids, 0, rows, lax.axis_index("group"))
    copies[1].wait()
    x = pick_rows(place, att[...])
    for i, block in enumerate(order):
        fetch(i, block).wait()
        if i + ahead < len(order):
            fetch(i + ahead, order[i + ahead]).start()
        elif i + ahead == len(order):
            late.start()
        y = jnp.dot(x, wbuf[i], preferred_element_type=f32).astype(bf16)
        obuf[i] = y
        if i >= chips:
            keep_acc[i - chips] = y[:cap]
        for copy in put(i):
            copy.start()
    late.wait()
    picked[...] = pick_rows(place, res[...])
    res_acc[...] = picked[:cap]
    last = pltpu.make_async_copy(picked.at[pl.ds(cap, rows - cap)], res_rest, small_sem.at[3])
    last.start()
    for i in range(2 * chips):
        for copy in put(i):
            copy.wait()
    last.wait()


def project(accept_rows, attention, residual, o_weight, chip_order, cap, width):
    rows, depth = attention.shape
    chips = len(chip_order)
    acc, rest = (chips, cap, width), (chips, rows - cap, width)
    return pl.pallas_call(
        functools.partial(project_kernel, chip_order, cap),
        in_specs=[HBM] * 4,
        out_specs=[HBM, VMEM, VMEM, HBM, HBM, HBM],
        out_shape=[
            pltpu.HBM(acc, bf16),
            jax.ShapeDtypeStruct(acc, bf16),
            jax.ShapeDtypeStruct(acc[1:], bf16),
            pltpu.HBM(rest, bf16),
            pltpu.HBM(rest, bf16),
            pltpu.HBM(rest[1:], bf16),
        ],
        scratch_shapes=[
            pltpu.VMEM(accept_rows.shape, i32),
            pltpu.VMEM(attention.shape, bf16),
            pltpu.VMEM(residual.shape, bf16),
            pltpu.VMEM(residual.shape, bf16),
            pltpu.VMEM((2 * chips, depth, width), bf16),
            pltpu.VMEM((2 * chips, rows, width), bf16),
            pltpu.SemaphoreType.DMA((3, 2 * chips)),
            pltpu.SemaphoreType.DMA((4,)),
        ],
        compiler_params=params(36),
        cost_estimate=cost(
            4 * rows * depth * width * chips, 4 * depth * width * chips + 4 * rows * width * chips
        ),
        name="project",
    )(*in_hbm(accept_rows, attention, residual, o_weight))


def pair_sums(keep, got, res):
    chips, rows, width = keep.shape

    def kernel(keep_ref, got_ref, res_ref, own_out, *outs):
        own_out[...] = (
            res_ref[...].astype(f32) + keep_ref[0].astype(f32) + got_ref[0].astype(f32)
        )
        for i, out in enumerate(outs):
            out[...] = (keep_ref[i + 1].astype(f32) + got_ref[i + 1].astype(f32)).astype(bf16)

    return pl.pallas_call(
        kernel,
        in_specs=[VMEM] * 3,
        out_specs=[VMEM] * chips,
        out_shape=[jax.ShapeDtypeStruct((rows, width), f32)]
        + [jax.ShapeDtypeStruct((rows, width), bf16)] * (chips - 1),
        compiler_params=params(8),
        cost_estimate=cost(chips * rows * width, 6 * chips * rows * width),
        name="pair_sums",
    )(keep, got, res)


def top_rows(own, came, first):
    rows, width = own.shape
    shapes = [(1, rows, width)] + ([(1, first, width)] if rows > first else [])

    def kernel(own_ref, *refs):
        total = own_ref[...]
        for ref in refs[: len(came)]:
            total = total + ref[...].astype(f32)
        for out in refs[len(came) :]:
            out[0] = total[: out.shape[1]].astype(bf16)

    return pl.pallas_call(
        kernel,
        in_specs=[VMEM] * (1 + len(came)),
        out_specs=[VMEM] * len(shapes),
        out_shape=[jax.ShapeDtypeStruct(s, bf16) for s in shapes],
        compiler_params=params(8),
        cost_estimate=cost(4 * rows * width, 12 * rows * width),
        name="top_rows",
    )(own, *came)


def start_of(counts_ref, replica):
    total = jnp.int32(0)
    for s in range(counts_ref.shape[0]):
        total = total + jnp.where(s < replica, counts_ref[s], 0)
    return total


def busiest_of(counts_ref):
    best, where = counts_ref[0], jnp.int32(0)
    for s in range(1, counts_ref.shape[0]):
        more = counts_ref[s] > best
        best = jnp.where(more, counts_ref[s], best)
        where = jnp.where(more, jnp.int32(s), where)
    return where


def rows_here(accepted, columns):
    p = iota((accepted, columns), 0) + (lax.axis_index("tensor") % 2) * (accepted // 2)
    return jnp.where(p >= accepted, p - accepted, p)


def destination(counts_ref, replica, k):
    return jnp.where(k < counts_ref[replica], start_of(counts_ref, replica) + k, -1)


def join_call(counts, gathered, extra, weight, so_far, common, cap, accepted):
    groups = len(gathered)
    thirds, _, width = gathered[0].shape
    features = weight.shape[-1]
    half = accepted // 2
    has_extra = extra is not None
    final = so_far is not None
    columns = groups * common + (cap - common if has_extra else 0)

    def kernel(counts_ref, *refs):
        refs = list(refs)
        blocks = [refs.pop(0) for _ in range(groups + has_extra)]
        so_far_ref = refs.pop(0) if final else None
        w_ref = refs.pop(0)
        rows_out = refs.pop(0)
        if final:
            *outs, joined = refs
            weights = [w_ref]
        else:
            *outs, joined, wbuf, wsem = refs
            weights = [wbuf.at[i] for i in range(thirds)]
            landing = weights + [outs[1]]
            copies = [
                pltpu.make_async_copy(w_ref.at[i], ref, wsem.at[i])
                for i, ref in enumerate(landing)
            ]
            copies[0].start()
            copies[1].start()
        g = lax.axis_index("group")
        j = iota((8, columns), 1)
        goes = jnp.full((8, columns), -1, i32)
        for back in range(groups):
            replica = g ^ back
            inside = (j >= back * common) & (j < (back + 1) * common)
            goes = jnp.where(inside, destination(counts_ref, replica, j - back * common), goes)
        if has_extra:
            k = j - groups * common + common
            goes = jnp.where(
                j >= groups * common, destination(counts_ref, busiest_of(counts_ref), k), goes
            )
        place = hit(rows_here(accepted, columns) == goes[:1])
        total = so_far_ref[...] if final else None
        for i in range(thirds):
            for back in range(groups):
                joined[i, back * common : (back + 1) * common] = blocks[back][i, :common]
            if has_extra:
                joined[i, groups * common :] = blocks[groups][i]
            x = jnp.dot(place, joined[i], preferred_element_type=f32).astype(bf16)
            rows_out[i] = x
            if not final:
                copies[i].wait()
                if i == 0:
                    copies[thirds].start()
            y = jnp.dot(x, weights[i][...], preferred_element_type=f32)
            total = y if total is None else total + y
        if final:
            outs[0][...] = total[:half]
            outs[1][...] = total[half:].astype(bf16)
        else:
            outs[0][...] = total
            copies[thirds].wait()

    rows_shape = jax.ShapeDtypeStruct((thirds, accepted, width), bf16)
    if final:
        out_shape = [
            rows_shape,
            jax.ShapeDtypeStruct((half, features), f32),
            jax.ShapeDtypeStruct((half, features), bf16),
        ]
    else:
        out_shape = [
            rows_shape,
            jax.ShapeDtypeStruct((accepted, features), f32),
            jax.ShapeDtypeStruct((width, features), bf16),
        ]
    operands = [counts, *gathered]
    if has_extra:
        operands.append(extra)
    if final:
        operands.append(so_far)
    return pl.pallas_call(
        kernel,
        in_specs=[SMEM] + [VMEM] * (len(operands) - 1) + [VMEM if final else HBM],
        out_specs=[VMEM] * len(out_shape),
        out_shape=out_shape,
        scratch_shapes=[pltpu.VMEM((thirds, columns, width), bf16)]
        + (
            []
            if final
            else [
                pltpu.VMEM((thirds, width, features), bf16),
                pltpu.SemaphoreType.DMA((thirds + 1,)),
            ]
        ),
        compiler_params=params(12 if final else 20),
        cost_estimate=cost(
            2 * thirds * accepted * width * features, 2 * thirds * width * features
        ),
        name="join_late" if final else "join_early",
    )(*operands, weight if final else in_hbm(weight)[0])


def goal_kernel(slots, cap, accepted, counts_ref, owners_ref, *refs):
    *sources, mine_out, other_out, held_targets, sem = refs
    targets = [held_targets.at[m] for m in range(len(sources))]
    copies = [
        pltpu.make_async_copy(ref, held_targets.at[m], sem.at[m])
        for m, ref in enumerate(sources)
    ]
    for copy in copies:
        copy.start()
    groups = owners_ref.shape[0]
    share = targets[0].shape[0]
    half = accepted // 2
    t = lax.axis_index("tensor")
    before = hit(iota((cap, cap), 0) < iota((cap, cap), 1))
    picks = [None] * len(targets)
    for g in range(groups):
        own = owners_ref[g : g + 1, :cap]
        mark = hit(iota((max(groups, 8), cap), 0) == own)
        prefix = jnp.dot(mark, before, preferred_element_type=f32)
        rank = jnp.sum(prefix * mark.astype(f32), axis=0, keepdims=True).astype(i32)
        slot = own * cap + g * slots + rank
        goes = destination(counts_ref, g, iota((8, cap), 1))
        place = hit(rows_here(accepted, cap) == goes[:1])
        for m in range(len(targets)):
            held = iota((share, cap), 0) + (t ^ (2 * m)) * share
            z = lax.dot_general(
                place, hit(held == slot), (((1,), (1,)), ((), ())), preferred_element_type=f32
            )
            picks[m] = z if picks[m] is None else picks[m] + z
    total = None
    for m, ref in enumerate(targets):
        copies[m].wait()
        y = jnp.dot(picks[m].astype(bf16), ref[...], preferred_element_type=f32)
        total = y if total is None else total + y
    mine_out[...] = total[:half].astype(bf16)
    other_out[...] = total[half:].astype(bf16)


def goals(counts, owners, targets, slots, cap, accepted):
    features = targets[0].shape[1]
    return pl.pallas_call(
        functools.partial(goal_kernel, slots, cap, accepted),
        in_specs=[SMEM, VMEM] + [HBM] * len(targets),
        out_specs=[VMEM, VMEM],
        out_shape=[jax.ShapeDtypeStruct((accepted // 2, features), bf16)] * 2,
        scratch_shapes=[
            pltpu.VMEM((len(targets),) + targets[0].shape, bf16),
            pltpu.SemaphoreType.DMA((len(targets),)),
        ],
        compiler_params=params(28),
        cost_estimate=cost(2 * accepted * accepted * features, 4 * accepted * features),
        name="goals",
    )(counts, owners, *in_hbm(*targets))


def gauge(pieces, arrived, goal, goal_came, gain):
    half, part = pieces[0].shape
    n = len(pieces)
    features = part * n

    def kernel(*refs):
        piece_refs, came_refs = refs[:n], refs[n : 2 * n]
        goal_ref, goal_came_ref, gain_ref, c_out, goal_out, stats_out = refs[2 * n :]
        sums = [0.0, 0.0, 0.0]
        for i in range(n):
            at = slice(i * part, (i + 1) * part)
            c = piece_refs[i][...] + came_refs[i][...].astype(f32)
            goal = goal_ref[:, at].astype(f32) + goal_came_ref[:, at].astype(f32)
            gc = gain_ref[:, at] * c
            c_out[:, at] = c
            goal_out[:, at] = goal
            for k, v in enumerate((c * c, gc * gc, gc * goal)):
                sums[k] = sums[k] + jnp.sum(v, axis=1, keepdims=True)
        lane = iota((half, 128), 1)
        stats = jnp.zeros((half, 128), f32)
        for k in range(3):
            stats = jnp.where(lane == k, sums[k], stats)
        stats_out[...] = stats.T[:8]

    whole = jax.ShapeDtypeStruct((half, features), f32)
    return pl.pallas_call(
        kernel,
        in_specs=[VMEM] * (2 * n + 3),
        out_specs=[VMEM] * 3,
        out_shape=[whole, whole, jax.ShapeDtypeStruct((8, half), f32)],
        compiler_params=params(16),
        cost_estimate=cost(10 * half * features, 20 * half * features),
        name="gauge",
    )(*pieces, *arrived, goal, goal_came, gain)


def backward(counts, c, goal, gain, stats, width):
    half, features = c.shape
    n = len(stats)

    def kernel(counts_ref, c_ref, goal_ref, gain_ref, *refs):
        total = counts_ref[0]
        for s in range(1, counts_ref.shape[0]):
            total = total + counts_ref[s]
        inverse = 1.0 / jnp.full((half, 1), total, i32).astype(f32)
        sums = refs[0][...]
        for ref in refs[1:n]:
            sums = sums + ref[...]
        sums = jnp.concatenate([sums, jnp.zeros((120, half), f32)], axis=0).T
        squares, gained, crossed = sums[:, 0:1], sums[:, 1:2], sums[:, 2:3]
        scale = lax.rsqrt(squares / width + epsilon)
        inner = (scale * gained - crossed) * inverse
        gain = gain_ref[...]
        c = c_ref[...]
        slope = (c * scale * gain - goal_ref[...]) * inverse
        out = scale * gain * slope - c * (scale * scale * scale * inner / width)
        refs[n][...] = out.astype(bf16)

    return pl.pallas_call(
        kernel,
        in_specs=[SMEM] + [VMEM] * (3 + n),
        out_specs=VMEM,
        out_shape=jax.ShapeDtypeStruct((half, features), bf16),
        compiler_params=params(16),
        cost_estimate=cost(10 * half * features, 10 * half * features),
        name="backward",
    )(counts, c, goal, gain, *stats)


def finish(accept_rows, top_acc, base, arrivals, early_c, late_c, back, other):
    cap, width = top_acc.shape
    rows = accept_rows.shape[1]
    accepted = early_c.shape[1]
    half, features = back.shape
    thirds = early_c.shape[0] + late_c.shape[0]
    arrays = [array for part in arrivals for array, _ in part]
    block = min(256, width)
    per = width // block
    slots = 4

    def kernel(rows_ref, acc_ref, base_ref, *refs):
        refs = list(refs)
        came = [refs.pop(0) for _ in arrays]
        early_ref, late_ref, back_ref, other_ref, top_out, grad_out = refs[:6]
        backs, obuf, sem = refs[6:]
        backs[:half] = back_ref[...]
        backs[half:] = other_ref[...]

        def put(n):
            third, b = divmod(n, per)
            return pltpu.make_async_copy(
                obuf.at[n % slots],
                grad_out.at[third, pl.ds(b * block, block)],
                sem.at[n % slots],
            )

        steps = thirds * per
        for n in range(steps):
            third, b = divmod(n, per)
            ref = early_ref.at[third] if third < early_c.shape[0] else late_ref.at[0]
            if n >= slots:
                put(n - slots).wait()
            obuf[n % slots] = lax.dot_general(
                ref[:, b * block : (b + 1) * block],
                backs[...],
                (((0,), (0,)), ((), ())),
                preferred_element_type=f32,
            )
            put(n).start()
        place = place_of(rows_ref, 0, rows, lax.axis_index("group"))
        y = jnp.dot(place[:, :cap], acc_ref[...], preferred_element_type=f32)
        at = cap
        came = iter(came)
        for part in arrivals:
            size = part[0][0].shape[1]
            v = base_ref[at - cap : at - cap + size]
            for _, i in part:
                v = v + next(came)[i].astype(f32)
            y = y + jnp.dot(
                place[:, at : at + size], v.astype(bf16), preferred_element_type=f32
            )
            at += size
        top_out[...] = y.astype(bf16)
        for n in range(max(0, steps - slots), steps):
            put(n).wait()

    return pl.pallas_call(
        kernel,
        in_specs=[VMEM] * (7 + len(arrays)),
        out_specs=[VMEM, HBM],
        out_shape=[
            jax.ShapeDtypeStruct((rows, width), bf16),
            jax.ShapeDtypeStruct((thirds, width, features), f32),
        ],
        scratch_shapes=[
            pltpu.VMEM((accepted, features), bf16),
            pltpu.VMEM((slots, block, features), f32),
            pltpu.SemaphoreType.DMA((slots,)),
        ],
        compiler_params=params(24),
        cost_estimate=cost(
            2 * accepted * thirds * width * features, 4 * thirds * width * features
        ),
        name="finish",
    )(accept_rows, top_acc, base, *arrays, early_c, late_c, back, other)


def shards(
    low_state,
    mid_state,
    residual,
    attention,
    o_weight,
    fc_weight,
    norm_gain,
    target,
    counts,
    accept_rows,
    owners,
):
    groups = lax.axis_size("group")
    tensors = lax.axis_size("tensor")
    g = lax.axis_index("group")
    chips = tensors // 2
    rows, width = low_state.shape
    out_features = fc_weight.shape[2]
    train_rows = target.shape[0] * tensors
    slots = train_rows // (groups * groups)
    cap = groups * slots
    accepted = train_rows // 2
    common = min(cap, accepted - cap - (groups - 2) * slots)
    bits = [1 << i for i in range(1, tensors.bit_length() - 1)]
    group_bits = [1 << i for i in range(groups.bit_length() - 1)]

    def swap(x, mask):
        return lax.ppermute(x, "tensor", [(i, i ^ mask) for i in range(tensors)])

    def cross(x, mask):
        return lax.ppermute(x, "group", [(i, i ^ mask) for i in range(groups)])

    busiest = jnp.argmax(counts).astype(i32)

    def gather(full, first):
        blocks = [full, cross(full, 1)]
        blocks += [cross(first, mask) for mask in range(2, groups)]
        if cap == common:
            return blocks, None
        extra = jnp.where(
            ((busiest ^ g) & 1) != 0, blocks[1][:, common:], full[:, common:]
        )
        for bit in group_bits[1:]:
            other = cross(extra, bit)
            extra = jnp.where(((busiest ^ g) & bit) != 0, other, extra)
        return blocks, extra

    early = early_rows(accept_rows, low_state, mid_state, common, cap)
    early_all, early_extra = gather(early[0], early[-1])

    targets = [target] + [swap(target, 2 * m) for m in range(1, chips)]

    gray = [i ^ (i >> 1) for i in range(chips)]
    at = {m: i for i, m in enumerate(gray)}
    give_acc, keep_acc, res_acc, give_rest, keep_rest, res_rest = project(
        accept_rows, attention, residual, o_weight, gray, cap, width
    )
    got_acc = swap(give_acc, 1)
    got_rest = swap(give_rest, 1)

    own, *others = pair_sums(keep_acc, got_acc, res_acc)
    came = [swap(others[i - 1], 2 * gray[i]) for i in range(1, chips)]
    late = top_rows(own, came, common)
    top_acc = late[0][0]
    late_all, late_extra = gather(late[0], late[-1])

    n_rest = rows - cap
    base = res_rest.astype(f32) + keep_rest[0].astype(f32) + got_rest[0].astype(f32)
    arrivals = []
    for part, order in enumerate((bits, bits[::-1])):
        lo, hi = part * (n_rest // 2), (part + 1) * (n_rest // 2)
        arrived = {m: [] for m in range(chips)}

        def value(ms):
            ps = [at[m] for m in ms]
            if not any(arrived[m] for m in ms) and ps == list(range(ps[0], ps[0] + len(ps))):
                a = slice(ps[0], ps[0] + len(ps))
                return keep_rest[a, lo:hi].astype(f32) + got_rest[a, lo:hi].astype(f32)
            vals = []
            for m in ms:
                v = keep_rest[at[m], lo:hi].astype(f32) + got_rest[at[m], lo:hi].astype(f32)
                for array, i in arrived[m]:
                    v = v + array[i].astype(f32)
                vals.append(v)
            return jnp.stack(vals)

        held = list(range(chips))
        for bit in order:
            going = sorted((m for m in held if 2 * m & bit), key=lambda m: at[m])
            sent = value(going).astype(bf16)
            came = swap(sent, bit)
            for i, m in enumerate(going):
                arrived[m ^ (bit >> 1)].append((came, i))
            held = [m for m in held if not 2 * m & bit]
        arrivals.append(arrived[0])

    early_c, partial, late_weight = join_call(
        counts, early_all, early_extra, fc_weight, None, common, cap, accepted
    )
    late_c, mine, other = join_call(
        counts, late_all, late_extra, late_weight, partial, common, cap, accepted
    )

    goal, goal_other = goals(counts, owners, targets, slots, cap, accepted)
    goal_came = swap(goal_other, 1)

    mine = mine + swap(other, 1).astype(f32)
    pieces, arrived = [], []
    for part, order in enumerate((bits, bits[::-1])):
        lo = part * (out_features // 2)
        piece = mine[:, lo : lo + out_features // 2]
        for step, bit in enumerate(order):
            came = swap(piece.astype(bf16), bit)
            if step < len(order) - 1:
                piece = piece + came.astype(f32)
        pieces.append(piece)
        arrived.append(came)

    gain = norm_gain.astype(f32)[None, :]
    c, goal, stats = gauge(pieces, arrived, goal, goal_came, gain)
    all_stats = [stats] + [cross(stats, mask) for mask in range(1, groups)]
    back = backward(counts, c, goal, gain, all_stats, out_features * groups)
    other = swap(back, 1)
    top_state, grad = finish(
        accept_rows, top_acc, base, arrivals, early_c, late_c, back, other
    )
    return (top_state, grad)


def solution(mesh):
    in_specs = (
        P("group", "tensor"),
        P("group", "tensor"),
        P("group", "tensor"),
        P("group", "tensor"),
        P("tensor", None),
        P(None, "tensor", "group"),
        P("group"),
        P("tensor", "group"),
        P(),
        P(),
        P(),
    )
    out_specs = (P("group", "tensor"), P(None, "tensor", "group"))

    return jax.shard_map(shards, mesh=mesh, in_specs=in_specs, out_specs=out_specs, check_vma=False)
```

```python
import functools

import jax
import jax.numpy as jnp
from jax import lax
from jax.experimental import pallas as pl
from jax.experimental.pallas import tpu as pltpu
from jax.sharding import PartitionSpec as P


epsilon = 1e-05
f32 = jnp.float32
bf16 = jnp.bfloat16
i32 = jnp.int32


VMEM = pl.BlockSpec(memory_space=pltpu.VMEM)
SMEM = pl.BlockSpec(memory_space=pltpu.SMEM)
HBM = pl.BlockSpec(memory_space=pltpu.HBM)


def iota(shape, dim):
    return lax.broadcasted_iota(i32, shape, dim)


def cost(flops, read):
    return pl.CostEstimate(flops=int(flops), bytes_accessed=int(read), transcendentals=0)


def params(mib=56):
    return pltpu.CompilerParams(vmem_limit_bytes=mib << 20)


def in_hbm(*arrays):
    return [pltpu.with_memory_space_constraint(x, pltpu.HBM) for x in arrays]


def fetch_all(pairs, sems):
    copies = [
        pltpu.make_async_copy(src, dst, sems.at[i]) for i, (src, dst) in enumerate(pairs)
    ]
    for copy in copies:
        copy.start()
    return copies


def hit(cond):
    return jnp.where(cond, 1.0, 0.0).astype(bf16)


def place_of(rows_ref, lo, hi, replica):
    groups, rows = rows_ref.shape
    ids = jnp.where(iota((groups, hi - lo), 0) == replica, rows_ref[:, lo:hi], 0)
    ids = jnp.sum(ids, axis=0, keepdims=True)
    return hit(iota((rows, hi - lo), 0) == ids)


def pick_rows(place, x):
    return lax.dot_general(
        place, x, (((0,), (0,)), ((), ())), preferred_element_type=f32
    ).astype(bf16)


def early_kernel(rows_ref, low_ref, mid_ref, *refs):
    *outs, ids, buf, sem = refs
    copies = fetch_all([(rows_ref, ids), (low_ref, buf.at[0]), (mid_ref, buf.at[1])], sem)
    copies[0].wait()
    place = place_of(ids, 0, outs[0].shape[1], lax.axis_index("group"))
    for i in range(2):
        copies[1 + i].wait()
        got = pick_rows(place, buf[i])
        for out in outs:
            out[i] = got[: out.shape[1]]


def early_rows(accept_rows, low, mid, common, cap):
    rows, width = low.shape
    shapes = [(2, cap, width)] + ([(2, common, width)] if cap > common else [])
    return pl.pallas_call(
        early_kernel,
        in_specs=[HBM] * 3,
        out_specs=[VMEM] * len(shapes),
        out_shape=[jax.ShapeDtypeStruct(s, bf16) for s in shapes],
        scratch_shapes=[
            pltpu.VMEM(accept_rows.shape, i32),
            pltpu.VMEM((2, rows, width), bf16),
            pltpu.SemaphoreType.DMA((3,)),
        ],
        compiler_params=params(8),
        cost_estimate=cost(4 * rows * width * cap, 4 * rows * width + 4 * cap * width),
        name="early_rows",
    )(*in_hbm(accept_rows, low, mid))


def weight_blocks(order, w_ref, weights, sem):
    t = lax.axis_index("tensor")
    width = weights.shape[2]
    copies = []
    for i, block in enumerate(order):
        at = pl.ds(pl.multiple_of((t ^ block) * width, 128), width)
        copies.append(pltpu.make_async_copy(w_ref.at[:, at], weights.at[i], sem.at[i]))
    return copies


ahead = 3


def project_kernel(
    chip_order,
    rows_ref,
    att_ref,
    res_ref,
    w_ref,
    give,
    keep,
    res_rest,
    x_rest,
    ids,
    att,
    res,
    sent,
    picked,
    weights,
    sem,
    put_sem,
    small_sem,
):
    chips = len(chip_order)
    cap = keep.shape[1]
    order = [2 * m + 1 for m in chip_order] + [2 * m for m in chip_order]
    fetch = weight_blocks(order, w_ref, weights, sem)

    def put(i):
        return pltpu.make_async_copy(sent.at[i], give.at[i], put_sem.at[i])

    copies = fetch_all([(rows_ref, ids), (att_ref, att), (res_ref, res)], small_sem)
    for copy in fetch[:ahead]:
        copy.start()
    copies[0].wait()
    place = place_of(ids, 0, att.shape[0], lax.axis_index("group"))
    copies[1].wait()
    x = pick_rows(place[:, :cap], att[...])
    puts = [
        pltpu.make_async_copy(picked.at[0], x_rest, small_sem.at[3]),
        pltpu.make_async_copy(picked.at[1], res_rest, small_sem.at[4]),
    ]
    for i, copy in enumerate(fetch):
        if i == 1:
            picked[0] = pick_rows(place[:, cap:], att[...])
            puts[0].start()
        if i == 2:
            copies[2].wait()
            keep[chips] = pick_rows(place[:, :cap], res[...])
        if i == 3:
            picked[1] = pick_rows(place[:, cap:], res[...])
            puts[1].start()
        copy.wait()
        if i + ahead < len(fetch):
            fetch[i + ahead].start()
        y = jnp.dot(x, weights[i], preferred_element_type=f32).astype(bf16)
        if i < chips:
            sent[i] = y
            put(i).start()
        else:
            keep[i - chips] = y
    for i in range(chips):
        put(i).wait()
    for copy in puts:
        copy.wait()


def project(accept_rows, attention, residual, o_weight, chip_order, cap, width):
    rows, depth = attention.shape
    chips = len(chip_order)
    return pl.pallas_call(
        functools.partial(project_kernel, chip_order),
        in_specs=[HBM] * 4,
        out_specs=[HBM, VMEM, HBM, HBM],
        out_shape=[
            pltpu.HBM((chips, cap, width), bf16),
            jax.ShapeDtypeStruct((chips + 1, cap, width), bf16),
            pltpu.HBM((rows - cap, width), bf16),
            pltpu.HBM((rows - cap, depth), bf16),
        ],
        scratch_shapes=[
            pltpu.VMEM(accept_rows.shape, i32),
            pltpu.VMEM(attention.shape, bf16),
            pltpu.VMEM(residual.shape, bf16),
            pltpu.VMEM((chips, cap, width), bf16),
            pltpu.VMEM((2, rows - cap, width), bf16),
            pltpu.VMEM((2 * chips, depth, width), bf16),
            pltpu.SemaphoreType.DMA((2 * chips,)),
            pltpu.SemaphoreType.DMA((chips,)),
            pltpu.SemaphoreType.DMA((5,)),
        ],
        compiler_params=params(28),
        cost_estimate=cost(4 * cap * depth * width * chips, 4 * depth * width * chips),
        name="project",
    )(*in_hbm(accept_rows, attention, residual, o_weight))


def project_rest(x, o_weight, chip_order, width):
    rows, depth = x.shape
    chips = len(chip_order)
    blocks = 2 * chips
    order = [2 * m + 1 for m in chip_order] + [2 * m for m in chip_order]

    def kernel(x_ref, w_ref, give, keep, held, sent, weights, sem, put_sem):
        fetch = weight_blocks(order, w_ref, weights, sem)
        puts = [
            pltpu.make_async_copy(
                sent.at[i], (give if i < chips else keep).at[i % chips], put_sem.at[i]
            )
            for i in range(blocks)
        ]
        first = pltpu.make_async_copy(x_ref, held, put_sem.at[blocks])
        first.start()
        for copy in fetch[:ahead]:
            copy.start()
        first.wait()
        for i, copy in enumerate(fetch):
            copy.wait()
            if i + ahead < blocks:
                fetch[i + ahead].start()
            sent[i] = jnp.dot(held[...], weights[i], preferred_element_type=f32).astype(bf16)
            puts[i].start()
        for copy in puts:
            copy.wait()

    shape = pltpu.HBM((chips, rows, width), bf16)
    return pl.pallas_call(
        kernel,
        in_specs=[HBM] * 2,
        out_specs=[HBM] * 2,
        out_shape=[shape, shape],
        scratch_shapes=[
            pltpu.VMEM((rows, depth), bf16),
            pltpu.VMEM((blocks, rows, width), bf16),
            pltpu.VMEM((blocks, depth, width), bf16),
            pltpu.SemaphoreType.DMA((blocks,)),
            pltpu.SemaphoreType.DMA((blocks + 1,)),
        ],
        compiler_params=params(28),
        cost_estimate=cost(2 * rows * depth * width * blocks, 2 * depth * width * blocks),
        name="project_rest",
    )(*in_hbm(x, o_weight))


def pair_sums(keep, got):
    chips, rows, width = got.shape

    def kernel(keep_ref, got_ref, own_out, *outs):
        own_out[...] = (
            keep_ref[chips].astype(f32) + keep_ref[0].astype(f32) + got_ref[0].astype(f32)
        )
        for i, out in enumerate(outs):
            out[...] = (keep_ref[i + 1].astype(f32) + got_ref[i + 1].astype(f32)).astype(bf16)

    return pl.pallas_call(
        kernel,
        in_specs=[VMEM] * 2,
        out_specs=[VMEM] * chips,
        out_shape=[jax.ShapeDtypeStruct((rows, width), f32)]
        + [jax.ShapeDtypeStruct((rows, width), bf16)] * (chips - 1),
        compiler_params=params(8),
        cost_estimate=cost(chips * rows * width, 6 * chips * rows * width),
        name="pair_sums",
    )(keep, got)


def top_rows(own, came, first):
    rows, width = own.shape
    spans = [(0, rows)] + ([(0, first), (first, rows)] if rows > first else [])

    def kernel(own_ref, *refs):
        total = own_ref[...]
        for ref in refs[: len(came)]:
            total = total + ref[...].astype(f32)
        for (lo, hi), out in zip(spans, refs[len(came) :]):
            out[0] = total[lo:hi].astype(bf16)

    return pl.pallas_call(
        kernel,
        in_specs=[VMEM] * (1 + len(came)),
        out_specs=[VMEM] * len(spans),
        out_shape=[jax.ShapeDtypeStruct((1, hi - lo, width), bf16) for lo, hi in spans],
        compiler_params=params(8),
        cost_estimate=cost(4 * rows * width, 12 * rows * width),
        name="top_rows",
    )(own, *came)


def start_of(counts_ref, replica):
    total = jnp.int32(0)
    for s in range(counts_ref.shape[0]):
        total = total + jnp.where(s < replica, counts_ref[s], 0)
    return total


def busiest_of(counts_ref):
    best, where = counts_ref[0], jnp.int32(0)
    for s in range(1, counts_ref.shape[0]):
        more = counts_ref[s] > best
        best = jnp.where(more, counts_ref[s], best)
        where = jnp.where(more, jnp.int32(s), where)
    return where


def rows_here(accepted, columns):
    p = iota((accepted, columns), 0) + (lax.axis_index("tensor") % 2) * (accepted // 2)
    return jnp.where(p >= accepted, p - accepted, p)


def destination(counts_ref, replica, k):
    return jnp.where(k < counts_ref[replica], start_of(counts_ref, replica) + k, -1)


def join_call(counts, gathered, extra, weight, so_far, common, cap, accepted):
    groups = len(gathered)
    thirds, _, width = gathered[0].shape
    features = weight.shape[-1]
    half = accepted // 2
    has_extra = extra is not None
    final = so_far is not None
    columns = groups * common + (cap - common if has_extra else 0)

    def kernel(counts_ref, *refs):
        refs = list(refs)
        blocks = [refs.pop(0) for _ in range(groups + 2 * has_extra)]
        so_far_ref = refs.pop(0) if final else None
        w_ref = refs.pop(0)
        rows_out = refs.pop(0)
        if final:
            *outs, joined = refs
            weights = [w_ref]
        else:
            *outs, joined, wbuf, wsem = refs
            weights = [wbuf.at[i] for i in range(thirds)]
            landing = weights + [outs[1]]
            copies = [
                pltpu.make_async_copy(w_ref.at[i], ref, wsem.at[i])
                for i, ref in enumerate(landing)
            ]
            copies[0].start()
            copies[1].start()
        g = lax.axis_index("group")
        j = iota((8, columns), 1)
        goes = jnp.full((8, columns), -1, i32)
        for back in range(groups):
            replica = g ^ back
            inside = (j >= back * common) & (j < (back + 1) * common)
            goes = jnp.where(inside, destination(counts_ref, replica, j - back * common), goes)
        if has_extra:
            k = j - groups * common + common
            goes = jnp.where(
                j >= groups * common, destination(counts_ref, busiest_of(counts_ref), k), goes
            )
        place = hit(rows_here(accepted, columns) == goes[:1])
        total = so_far_ref[...] if final else None
        for i in range(thirds):
            for back in range(groups):
                joined[i, back * common : (back + 1) * common] = blocks[back][i, :common]
            if has_extra:
                crossed = ((busiest_of(counts_ref) ^ g) & (groups // 2)) != 0
                joined[i, groups * common :] = jnp.where(
                    crossed, blocks[groups + 1][i], blocks[groups][i]
                )
            x = jnp.dot(place, joined[i], preferred_element_type=f32).astype(bf16)
            rows_out[i] = x
            if not final:
                copies[i].wait()
                if i == 0:
                    copies[thirds].start()
            y = jnp.dot(x, weights[i][...], preferred_element_type=f32)
            total = y if total is None else total + y
        if final:
            outs[0][...] = total[:half]
            outs[1][...] = total[half:].astype(bf16)
        else:
            outs[0][...] = total
            copies[thirds].wait()

    rows_shape = jax.ShapeDtypeStruct((thirds, accepted, width), bf16)
    if final:
        out_shape = [
            rows_shape,
            jax.ShapeDtypeStruct((half, features), f32),
            jax.ShapeDtypeStruct((half, features), bf16),
        ]
    else:
        out_shape = [
            rows_shape,
            jax.ShapeDtypeStruct((accepted, features), f32),
            jax.ShapeDtypeStruct((width, features), bf16),
        ]
    operands = [counts, *gathered]
    if has_extra:
        operands.extend(extra)
    if final:
        operands.append(so_far)
    return pl.pallas_call(
        kernel,
        in_specs=[SMEM] + [VMEM] * (len(operands) - 1) + [VMEM if final else HBM],
        out_specs=[VMEM] * len(out_shape),
        out_shape=out_shape,
        scratch_shapes=[pltpu.VMEM((thirds, columns, width), bf16)]
        + (
            []
            if final
            else [
                pltpu.VMEM((thirds, width, features), bf16),
                pltpu.SemaphoreType.DMA((thirds + 1,)),
            ]
        ),
        compiler_params=params(12 if final else 20),
        cost_estimate=cost(
            2 * thirds * accepted * width * features, 2 * thirds * width * features
        ),
        name="join_late" if final else "join_early",
    )(*operands, weight if final else in_hbm(weight)[0])


def goal_kernel(slots, cap, accepted, counts_ref, owners_ref, *refs):
    *sources, mine_out, other_out, held_targets, sem = refs
    targets = [held_targets.at[m] for m in range(len(sources))]
    copies = [
        pltpu.make_async_copy(ref, held_targets.at[m], sem.at[m])
        for m, ref in enumerate(sources)
    ]
    for copy in copies:
        copy.start()
    groups = owners_ref.shape[0]
    share = targets[0].shape[0]
    half = accepted // 2
    t = lax.axis_index("tensor")
    before = hit(iota((cap, cap), 0) < iota((cap, cap), 1))
    picks = [None] * len(targets)
    for g in range(groups):
        own = owners_ref[g : g + 1, :cap]
        mark = hit(iota((max(groups, 8), cap), 0) == own)
        prefix = jnp.dot(mark, before, preferred_element_type=f32)
        rank = jnp.sum(prefix * mark.astype(f32), axis=0, keepdims=True).astype(i32)
        slot = own * cap + g * slots + rank
        goes = destination(counts_ref, g, iota((8, cap), 1))
        place = hit(rows_here(accepted, cap) == goes[:1])
        for m in range(len(targets)):
            held = iota((share, cap), 0) + (t ^ (2 * m)) * share
            z = lax.dot_general(
                place, hit(held == slot), (((1,), (1,)), ((), ())), preferred_element_type=f32
            )
            picks[m] = z if picks[m] is None else picks[m] + z
    total = None
    for m, ref in enumerate(targets):
        copies[m].wait()
        y = jnp.dot(picks[m].astype(bf16), ref[...], preferred_element_type=f32)
        total = y if total is None else total + y
    mine_out[...] = total[:half].astype(bf16)
    other_out[...] = total[half:].astype(bf16)


def goals(counts, owners, targets, slots, cap, accepted):
    features = targets[0].shape[1]
    return pl.pallas_call(
        functools.partial(goal_kernel, slots, cap, accepted),
        in_specs=[SMEM, VMEM] + [HBM] * len(targets),
        out_specs=[VMEM, VMEM],
        out_shape=[jax.ShapeDtypeStruct((accepted // 2, features), bf16)] * 2,
        scratch_shapes=[
            pltpu.VMEM((len(targets),) + targets[0].shape, bf16),
            pltpu.SemaphoreType.DMA((len(targets),)),
        ],
        compiler_params=params(28),
        cost_estimate=cost(2 * accepted * accepted * features, 4 * accepted * features),
        name="goals",
    )(counts, owners, *in_hbm(*targets))


def gauge(pieces, arrived, goal, goal_came, gain):
    half, part = pieces[0].shape
    n = len(pieces)
    features = part * n

    def kernel(*refs):
        piece_refs, came_refs = refs[:n], refs[n : 2 * n]
        goal_ref, goal_came_ref, gain_ref, c_out, goal_out, stats_out = refs[2 * n :]
        sums = [0.0, 0.0, 0.0]
        for i in range(n):
            at = slice(i * part, (i + 1) * part)
            c = piece_refs[i][...] + came_refs[i][...].astype(f32)
            goal = goal_ref[:, at].astype(f32) + goal_came_ref[:, at].astype(f32)
            gc = gain_ref[:, at] * c
            c_out[:, at] = c
            goal_out[:, at] = goal
            for k, v in enumerate((c * c, gc * gc, gc * goal)):
                sums[k] = sums[k] + jnp.sum(v, axis=1, keepdims=True)
        lane = iota((half, 128), 1)
        stats = jnp.zeros((half, 128), f32)
        for k in range(3):
            stats = jnp.where(lane == k, sums[k], stats)
        stats_out[...] = stats.T[:8]

    whole = jax.ShapeDtypeStruct((half, features), f32)
    return pl.pallas_call(
        kernel,
        in_specs=[VMEM] * (2 * n + 3),
        out_specs=[VMEM] * 3,
        out_shape=[whole, whole, jax.ShapeDtypeStruct((8, half), f32)],
        compiler_params=params(16),
        cost_estimate=cost(10 * half * features, 20 * half * features),
        name="gauge",
    )(*pieces, *arrived, goal, goal_came, gain)


def backward(counts, c, goal, gain, stats, width):
    half, features = c.shape
    n = len(stats)

    def kernel(counts_ref, c_ref, goal_ref, gain_ref, *refs):
        total = counts_ref[0]
        for s in range(1, counts_ref.shape[0]):
            total = total + counts_ref[s]
        inverse = 1.0 / jnp.full((half, 1), total, i32).astype(f32)
        sums = refs[0][...]
        for ref in refs[1:n]:
            sums = sums + ref[...]
        sums = jnp.concatenate([sums, jnp.zeros((120, half), f32)], axis=0).T
        squares, gained, crossed = sums[:, 0:1], sums[:, 1:2], sums[:, 2:3]
        scale = lax.rsqrt(squares / width + epsilon)
        inner = (scale * gained - crossed) * inverse
        gain = gain_ref[...]
        c = c_ref[...]
        slope = (c * scale * gain - goal_ref[...]) * inverse
        out = scale * gain * slope - c * (scale * scale * scale * inner / width)
        refs[n][...] = out.astype(bf16)

    return pl.pallas_call(
        kernel,
        in_specs=[SMEM] + [VMEM] * (3 + n),
        out_specs=VMEM,
        out_shape=jax.ShapeDtypeStruct((half, features), bf16),
        compiler_params=params(16),
        cost_estimate=cost(10 * half * features, 10 * half * features),
        name="backward",
    )(counts, c, goal, gain, *stats)


def finish(accept_rows, top_acc, base, arrivals, early_c, late_c, back, other):
    cap, width = top_acc.shape
    rows = accept_rows.shape[1]
    accepted = early_c.shape[1]
    half, features = back.shape
    thirds = early_c.shape[0] + late_c.shape[0]
    arrays = [array for part in arrivals for array, _ in part]
    block = min(256, width)
    per = width // block
    slots = 4

    def kernel(rows_ref, acc_ref, base_ref, *refs):
        refs = list(refs)
        came = [refs.pop(0) for _ in arrays]
        early_ref, late_ref, back_ref, other_ref, top_out, grad_out = refs[:6]
        backs, obuf, sem = refs[6:]
        backs[:half] = back_ref[...]
        backs[half:] = other_ref[...]

        def put(n):
            third, b = divmod(n, per)
            return pltpu.make_async_copy(
                obuf.at[n % slots],
                grad_out.at[third, pl.ds(b * block, block)],
                sem.at[n % slots],
            )

        steps = thirds * per
        for n in range(steps):
            third, b = divmod(n, per)
            ref = early_ref.at[third] if third < early_c.shape[0] else late_ref.at[0]
            if n >= slots:
                put(n - slots).wait()
            obuf[n % slots] = lax.dot_general(
                ref[:, b * block : (b + 1) * block],
                backs[...],
                (((0,), (0,)), ((), ())),
                preferred_element_type=f32,
            )
            put(n).start()
        place = place_of(rows_ref, 0, rows, lax.axis_index("group"))
        y = jnp.dot(place[:, :cap], acc_ref[...], preferred_element_type=f32)
        at = cap
        came = iter(came)
        for part in arrivals:
            size = part[0][0].shape[1]
            v = base_ref[at - cap : at - cap + size]
            for _, i in part:
                v = v + next(came)[i].astype(f32)
            y = y + jnp.dot(
                place[:, at : at + size], v.astype(bf16), preferred_element_type=f32
            )
            at += size
        top_out[...] = y.astype(bf16)
        for n in range(max(0, steps - slots), steps):
            put(n).wait()

    return pl.pallas_call(
        kernel,
        in_specs=[VMEM] * (7 + len(arrays)),
        out_specs=[VMEM, HBM],
        out_shape=[
            jax.ShapeDtypeStruct((rows, width), bf16),
            jax.ShapeDtypeStruct((thirds, width, features), f32),
        ],
        scratch_shapes=[
            pltpu.VMEM((accepted, features), bf16),
            pltpu.VMEM((slots, block, features), f32),
            pltpu.SemaphoreType.DMA((slots,)),
        ],
        compiler_params=params(24),
        cost_estimate=cost(
            2 * accepted * thirds * width * features, 4 * thirds * width * features
        ),
        name="finish",
    )(accept_rows, top_acc, base, *arrays, early_c, late_c, back, other)


def shards(
    low_state,
    mid_state,
    residual,
    attention,
    o_weight,
    fc_weight,
    norm_gain,
    target,
    counts,
    accept_rows,
    owners,
):
    groups = lax.axis_size("group")
    tensors = lax.axis_size("tensor")
    g = lax.axis_index("group")
    chips = tensors // 2
    rows, width = low_state.shape
    out_features = fc_weight.shape[2]
    train_rows = target.shape[0] * tensors
    slots = train_rows // (groups * groups)
    cap = groups * slots
    accepted = train_rows // 2
    common = min(cap, accepted - cap - (groups - 2) * slots)
    bits = [1 << i for i in range(1, tensors.bit_length() - 1)]
    group_bits = [1 << i for i in range(groups.bit_length() - 1)]

    def swap(x, mask):
        return lax.ppermute(x, "tensor", [(i, i ^ mask) for i in range(tensors)])

    def cross(x, mask):
        return lax.ppermute(x, "group", [(i, i ^ mask) for i in range(groups)])

    def gather(full, first, extra):
        blocks = [first if extra is not None else full]
        blocks += [cross(blocks[0], 1)]
        blocks += [cross(first, mask) for mask in range(2, groups)]
        if cap == common:
            return blocks, None
        if extra is None:
            other, extra = blocks[1][:, common:], full[:, common:]
        else:
            other = cross(extra, 1)
        busiest = jnp.argmax(counts).astype(i32)
        for bit, after in zip(group_bits, group_bits[1:]):
            extra = jnp.where(((busiest ^ g) & bit) != 0, other, extra)
            other = cross(extra, after)
        return blocks, (extra, other)

    early = early_rows(accept_rows, low_state, mid_state, common, cap)
    early_all, early_extra = gather(early[0], early[-1], None)

    targets = [target] + [swap(target, 2 * m) for m in range(1, chips)]

    gray = [i ^ (i >> 1) for i in range(chips)]
    at = {m: i for i, m in enumerate(gray)}
    give_acc, keep_acc, res_rest, x_rest = project(
        accept_rows, attention, residual, o_weight, gray, cap, width
    )
    give_rest, keep_rest = project_rest(x_rest, o_weight, gray, width)
    got_acc = swap(give_acc, 1)
    got_rest = swap(give_rest, 1)

    own, *others = pair_sums(keep_acc, got_acc)
    came = [swap(others[i - 1], 2 * gray[i]) for i in range(1, chips)]
    late = top_rows(own, came, common)
    top_acc = late[0][0]
    if cap > common:
        late_all, late_extra = gather(*late)
    else:
        late_all, late_extra = gather(late[0], late[0], None)

    n_rest = rows - cap
    base = res_rest.astype(f32) + keep_rest[0].astype(f32) + got_rest[0].astype(f32)
    arrivals = []
    for part, order in enumerate((bits, bits[::-1])):
        lo, hi = part * (n_rest // 2), (part + 1) * (n_rest // 2)
        arrived = {m: [] for m in range(chips)}

        def value(ms):
            ps = [at[m] for m in ms]
            if not any(arrived[m] for m in ms) and ps == list(range(ps[0], ps[0] + len(ps))):
                a = slice(ps[0], ps[0] + len(ps))
                return keep_rest[a, lo:hi].astype(f32) + got_rest[a, lo:hi].astype(f32)
            vals = []
            for m in ms:
                v = keep_rest[at[m], lo:hi].astype(f32) + got_rest[at[m], lo:hi].astype(f32)
                for array, i in arrived[m]:
                    v = v + array[i].astype(f32)
                vals.append(v)
            return jnp.stack(vals)

        held = list(range(chips))
        for bit in order:
            going = sorted((m for m in held if 2 * m & bit), key=lambda m: at[m])
            sent = value(going).astype(bf16)
            came = swap(sent, bit)
            for i, m in enumerate(going):
                arrived[m ^ (bit >> 1)].append((came, i))
            held = [m for m in held if not 2 * m & bit]
        arrivals.append(arrived[0])

    early_c, partial, late_weight = join_call(
        counts, early_all, early_extra, fc_weight, None, common, cap, accepted
    )
    late_c, mine, other = join_call(
        counts, late_all, late_extra, late_weight, partial, common, cap, accepted
    )

    goal, goal_other = goals(counts, owners, targets, slots, cap, accepted)
    goal_came = swap(goal_other, 1)

    mine = mine + swap(other, 1).astype(f32)
    pieces, arrived = [], []
    for part, order in enumerate((bits, bits[::-1])):
        lo = part * (out_features // 2)
        piece = mine[:, lo : lo + out_features // 2]
        for step, bit in enumerate(order):
            came = swap(piece.astype(bf16), bit)
            if step < len(order) - 1:
                piece = piece + came.astype(f32)
        pieces.append(piece)
        arrived.append(came)

    gain = norm_gain.astype(f32)[None, :]
    c, goal, stats = gauge(pieces, arrived, goal, goal_came, gain)
    all_stats = [stats] + [cross(stats, mask) for mask in range(1, groups)]
    back = backward(counts, c, goal, gain, all_stats, out_features * groups)
    other = swap(back, 1)
    top_state, grad = finish(
        accept_rows, top_acc, base, arrivals, early_c, late_c, back, other
    )
    return (top_state, grad)


def solution(mesh):
    in_specs = (
        P("group", "tensor"),
        P("group", "tensor"),
        P("group", "tensor"),
        P("group", "tensor"),
        P("tensor", None),
        P(None, "tensor", "group"),
        P("group"),
        P("tensor", "group"),
        P(),
        P(),
        P(),
    )
    out_specs = (P("group", "tensor"), P(None, "tensor", "group"))

    return jax.shard_map(shards, mesh=mesh, in_specs=in_specs, out_specs=out_specs, check_vma=False)
```
